128 devices in a mesh: req: 16 (over z, y), mlp: 8 (over x, core).
Axes of the slice: x: 4, y: 4, z: 4, core: 2. Of those that a mesh axis runs over, the one named last changes fastest.
Arguments:
- prompt_rows: bfloat16 [32768, 1792], P(('req', 'mlp')), may hold values from -6 to 6
- prompt_edge: bfloat16 [128, 2, 1792], P(('req', 'mlp')), may hold values from -6 to 6
- decode_rows: bfloat16 [512, 1792], P(('req', 'mlp')), may hold values from -6 to 6
- decode_edge: bfloat16 [512, 2, 1792], P(('req', 'mlp')), may hold values from -6 to 6
- decode_live: int32 [512], P(('req', 'mlp')), may hold values 0 or 1
- cache_length: int32 [512], P(('req', 'mlp')), may hold values from 1 to 32768, as said below
- cache_state: float32 [512, 273, 1792], P(('req', 'mlp')), as said below
- cache_keysum: float32 [512, 272, 16], P(('req', 'mlp')), as said below
- prefix_length: int32 [8], P('mlp'), may hold values from 256 to 2048, as said below
- prefix_state: float32 [8, 273, 1792], P('mlp', None, 'req'), as said below
- prefix_keysum: float32 [8, 272, 16], P('mlp', None, 'req'), as said below
- conv_gain: float32 [1792], replicated, may hold values from 0.5 to 1.5
- conv_taps: float32 [3, 1792], replicated, may hold values from -3 to 3
- attend_gain: float32 [1792], replicated, may hold values from 0.5 to 1.5
- feature_weight: bfloat16 [1792, 512], replicated, may hold values from -0.125 to 0.125
- value_weight: bfloat16 [1792, 1792], replicated, may hold values from -0.125 to 0.125
- output_weight: bfloat16 [1792, 1792], replicated, may hold values from -0.125 to 0.125
- hidden_gain: float32 [1792], replicated, may hold values from 0.5 to 1.5
- gate_up: bfloat16 [2, 1792, 3584], P(None, 'req', 'mlp'), may hold values from -0.125 to 0.125
- down_weight: bfloat16 [3584, 1792], P('mlp', 'req'), may hold values from -0.09375 to 0.09375
Outputs:
- prompt_out: bfloat16 [32768, 1792], P(('req', 'mlp'))
- decode_out: bfloat16 [512, 1792], P(('req', 'mlp'))
The draws below stay inside these ranges and needn't reach their ends.
Inputs may be any that keep to these rules, and one draw needn't show every extreme that they name: `cache_length`: every slot's length is at least 1; some slot holds exactly 32768 tokens. `cache_state`: drawn as cache_length times the mean of phi(k) v^T over a few sampled keys k and values v of each head, plus independent noise of size sqrt(cache_length). `cache_keysum`: drawn as cache_length times the mean of phi_rest over the same sampled keys, so that cache_length + phi_rest(q) . cache_keysum is a sum of positive terms. `prefix_length`: A multiple of 256; some group's prefix is exactly 2048 tokens. `prefix_state`: drawn as prefix_length times the mean of phi(k) v^T over a few sampled keys and values of each head, plus independent noise of size sqrt(prefix_length). `prefix_keysum`: prefix_length times the mean of phi_rest over the same sampled keys.
All inputs are finite; a program needn't handle non-finite values. No bound on the sum of `decode_live` on one device may be relied on, other than what follows from the above.
Results may differ from the reference program's by a relative error of at most 0.014.
Values may be sent and summed in bfloat16 or wider, within the bound.
A program may use at most 128 MiB of HBM per device.

```python
import jax
import jax.numpy as jnp
from jax import lax

D = 1792
H = 16
FD = 16
DV = 112
FF = 3584
NF = 273
PREFILL = 256
DEC = 4
CACHE_MAX = 32768
GROUPS = 8
PROMPT_ROWS = 32768
DECODES = 512
N_MLP = 8
DEVICES = 128


def long_lengths(key, row_count):
    exponent = jax.random.randint(jax.random.fold_in(key, 101), (row_count,), 0, 16)
    powers = jnp.left_shift(jnp.ones((row_count,), jnp.int32), exponent)
    offsets = jax.random.randint(jax.random.fold_in(key, 102), (row_count,), 0, 32768)
    lengths = jnp.minimum(powers + offsets % powers, CACHE_MAX)
    return lengths.at[0].set(CACHE_MAX)


def group_lengths(key):
    multiple = jax.random.randint(jax.random.fold_in(key, 201), (GROUPS,), 1, 9)
    return (PREFILL * multiple).at[0].set(8 * PREFILL)


def sample_features(key, row_count, salt):
    sampled = jax.random.normal(jax.random.fold_in(key, salt), (row_count, 4, H, FD), jnp.float32)
    linear = sampled * FD ** (-0.25)
    square = (sampled[..., :, None] * sampled[..., None, :]).reshape(row_count, 4, H, FD * FD) * (2.0 * FD) ** (-0.5)
    constant = jnp.ones((row_count, 4, H, 1), jnp.float32)
    return jnp.concatenate([constant, linear, square], axis=-1)


def key_sums(key, row_count, lengths, salt):
    features = sample_features(key, row_count, salt)[..., 1:]
    averaged = (features[:, 0] + features[:, 1] + features[:, 2] + features[:, 3]) * 0.25
    return jnp.transpose(averaged, (0, 2, 1)) * lengths.astype(jnp.float32)[:, None, None]


def state_sums(key, row_count, lengths, salt):
    features = sample_features(key, row_count, salt)
    values = jax.random.normal(jax.random.fold_in(key, salt + 7), (row_count, 4, H, DV), jnp.float32)
    total = jnp.zeros((row_count, NF, H, DV), jnp.float32)
    for sample_index in range(4):
        outer = features[:, sample_index][:, :, :, None] * values[:, sample_index][:, :, None, :]
        total = total + jnp.transpose(outer, (0, 2, 1, 3))
    scale_long = lengths.astype(jnp.float32)[:, None, None]
    noise = jax.random.normal(jax.random.fold_in(key, salt + 11), (row_count, NF, D), jnp.float32)
    return total.reshape(row_count, NF, D) * 0.25 * scale_long + noise * jnp.sqrt(scale_long)


def draw_cache_length(key, part):
    return long_lengths(key, DECODES)


def draw_cache_state(key, part):
    return state_sums(key, DECODES, long_lengths(key, DECODES), 301)


def draw_cache_keysum(key, part):
    return key_sums(key, DECODES, long_lengths(key, DECODES), 301)


def draw_prefix_length(key, part):
    return group_lengths(key)


def draw_prefix_state(key, part):
    return state_sums(key, GROUPS, group_lengths(key), 401)


def draw_prefix_keysum(key, part):
    return key_sums(key, GROUPS, group_lengths(key), 401)


def with_ends(drawn, rng, low, largest):
    extent = drawn.shape
    spot = [jax.random.randint(jax.random.fold_in(rng, axis), (), 0, extent[axis]) for axis in range(len(extent))]
    drawn = drawn.at[tuple(spot)].set(low)
    longest = extent.index(max(extent))
    spot[longest] = (spot[longest] + 1) % extent[longest]
    return drawn.at[tuple(spot)].set(largest)


def level_of(key, dims, pieces, least, top_value):
    def one(position, shards_of):
        draws = jax.random.uniform(jax.random.fold_in(jax.random.fold_in(key, 6), position), (shards_of,), jnp.float32, least / len(pieces), top_value / len(pieces))
        return jnp.repeat(jnp.exp(draws), dims[position] // shards_of).reshape((-1,) + (1,) * (len(dims) - position - 1))

    level = one(*pieces[0])
    for cut in pieces[1:]:
        level = level * one(*cut)
    return level


def scatter_about(stream_key, dims, scale, reach, split=(), kind=jnp.bfloat16):
    entries = jax.random.normal(stream_key, dims, jnp.float32) * scale
    if len(split) > 0:
        entries = level_of(stream_key, dims, split, -0.22, 0.18) * entries
    return jnp.clip(entries, min=-reach, max=reach).astype(kind)


def setup_inputs(seed: int = 0) -> dict:
    streams_of = jax.random.split(jax.random.key(seed), 21)
    return {
        "prompt_rows": scatter_about(streams_of[0], (PROMPT_ROWS, D), 1.0, 6.0, ((0, 128),)),
        "prompt_edge": scatter_about(streams_of[1], (DEVICES, 2, D), 1.0, 6.0, ((0, 128),)),
        "decode_rows": scatter_about(streams_of[2], (DECODES, D), 1.0, 6.0, ((0, 128),)),
        "decode_edge": scatter_about(streams_of[3], (DECODES, 2, D), 1.0, 6.0, ((0, 128),)),
        "decode_live": with_ends((jax.random.randint(streams_of[4], (DECODES,), 0, 4) < 3).astype(jnp.int32), jax.random.fold_in(streams_of[4], 1), 0, 1),
        "cache_length": draw_cache_length(jax.random.fold_in(streams_of[20], 71), 0),
        "cache_state": draw_cache_state(jax.random.fold_in(streams_of[20], 71), 0),
        "cache_keysum": draw_cache_keysum(jax.random.fold_in(streams_of[20], 71), 0),
        "prefix_length": draw_prefix_length(jax.random.fold_in(streams_of[20], 71), 0),
        "prefix_state": draw_prefix_state(jax.random.fold_in(streams_of[20], 71), 0),
        "prefix_keysum": draw_prefix_keysum(jax.random.fold_in(streams_of[20], 71), 0),
        "conv_gain": jnp.clip(1.0 + 0.1 * jax.random.normal(streams_of[11], (D,), jnp.float32), 0.5, 1.5),
        "conv_taps": scatter_about(streams_of[12], (3, D), 0.5, 3.0, (), jnp.float32),
        "attend_gain": jnp.clip(1.0 + 0.1 * jax.random.normal(streams_of[13], (D,), jnp.float32), 0.5, 1.5),
        "feature_weight": scatter_about(streams_of[14], (D, 2 * H * FD), D ** -0.5, 0.125),
        "value_weight": scatter_about(streams_of[15], (D, D), D ** -0.5, 0.125),
        "output_weight": scatter_about(streams_of[16], (D, D), D ** -0.5, 0.125),
        "hidden_gain": jnp.clip(1.0 + 0.1 * jax.random.normal(streams_of[17], (D,), jnp.float32), 0.5, 1.5),
        "gate_up": scatter_about(streams_of[18], (2, D, FF), D ** -0.5, 0.125, ((1, 16), (2, 8))),
        "down_weight": scatter_about(streams_of[19], (FF, D), FF ** -0.5, 0.09375, ((0, 8), (1, 16))),
    }


epsilon = 1e-06
highest = lax.Precision.HIGHEST

def root_norm(row_values, scale_gain):
    widened = row_values.astype(jnp.float32)
    return widened * lax.rsqrt(lax.optimization_barrier(jnp.mean(widened * widened, axis=-1, keepdims=True)) + epsilon) * scale_gain

def rounded(row_values):
    return lax.optimization_barrier(row_values.astype(jnp.bfloat16)).astype(jnp.float32)

def taylor_features(queries):
    linear = queries * FD ** (-0.25)
    square = (queries[..., :, None] * queries[..., None, :]).reshape(queries.shape[:-1] + (FD * FD,)) * (2.0 * FD) ** (-0.5)
    constant = jnp.ones(queries.shape[:-1] + (1,), jnp.float32)
    return jnp.concatenate([constant, linear, square], axis=-1)

def gated_conv(row_values, normed, before_two, before_one, conv_taps):
    convolved = conv_taps[0] * normed + conv_taps[1] * before_one + conv_taps[2] * before_two
    return (row_values.astype(jnp.float32) + convolved * jax.nn.sigmoid(normed)).astype(jnp.bfloat16)

def project(conv_out, attend_gain, feature_weight, value_weight):
    normed = root_norm(conv_out, attend_gain).astype(jnp.bfloat16)
    features = jnp.dot(normed, feature_weight, preferred_element_type=jnp.float32).astype(jnp.bfloat16)
    values = jnp.dot(normed, value_weight, preferred_element_type=jnp.float32).astype(jnp.bfloat16)
    row_count = conv_out.shape[0]
    query_rows = features[:, :H * FD].reshape(row_count, H, FD)
    key_rows = features[:, H * FD:].reshape(row_count, H, FD)
    return (query_rows, key_rows, values.reshape(row_count, H, DV))

def block_local(query_rows, key_rows, value_rows):
    row_count = query_rows.shape[0]
    scores = jnp.einsum('thf,shf->hts', query_rows.astype(jnp.float32), key_rows.astype(jnp.float32)) * FD ** (-0.5)
    row_index = lax.broadcasted_iota(jnp.int32, (row_count, row_count), 0)
    earlier = lax.broadcasted_iota(jnp.int32, (row_count, row_count), 1)
    weights = jnp.where(earlier <= row_index, 1.0 + scores + 0.5 * scores * scores, 0.0)
    denominator = lax.optimization_barrier(jnp.sum(weights, axis=-1)).T
    numerator = jnp.einsum('hts,shv->thv', rounded(weights), value_rows.astype(jnp.float32))
    return (numerator, denominator)

def decode_attend(query_rows, key_rows, value_rows, slot_state, slot_keysum, slot_length):
    row_count = query_rows.shape[0]
    queries = query_rows.astype(jnp.float32)
    scores = lax.optimization_barrier(jnp.sum(queries * key_rows.astype(jnp.float32), axis=-1)) * FD ** (-0.5)
    own_weight = 1.0 + scores + 0.5 * scores * scores
    lifted = taylor_features(queries)
    numerator = jnp.einsum('nhf,nfhv->nhv', lifted, slot_state.reshape(row_count, NF, H, DV), precision=highest)
    numerator = numerator + own_weight[..., None] * value_rows.astype(jnp.float32)
    denominator = slot_length.astype(jnp.float32)[:, None] + jnp.einsum('nhf,nfh->nh', lifted[..., 1:], slot_keysum, precision=highest) + own_weight
    return (numerator / denominator[..., None]).reshape(row_count, D).astype(jnp.bfloat16)

def feed_forward(attend_out, hidden_gain, gate_up, down_weight):
    row_count = attend_out.shape[0]
    normed = root_norm(attend_out, hidden_gain).astype(jnp.bfloat16)
    gate_rows = jnp.dot(normed, gate_up[0], preferred_element_type=jnp.float32)
    up_rows = jnp.dot(normed, gate_up[1], preferred_element_type=jnp.float32)
    hidden = (jax.nn.silu(gate_rows) * up_rows).astype(jnp.bfloat16)
    block_width = FF // N_MLP
    partials = jnp.einsum('nbu,bud->bnd', hidden.reshape(row_count, N_MLP, block_width).astype(jnp.float32), down_weight.reshape(N_MLP, block_width, D).astype(jnp.float32))
    summed = lax.optimization_barrier(jnp.sum(rounded(partials), axis=0))
    return (attend_out.astype(jnp.float32) + summed).astype(jnp.bfloat16)

def reference(prompt_rows, prompt_edge, decode_rows, decode_edge, decode_live, cache_length, cache_state, cache_keysum, prefix_length, prefix_state, prefix_keysum, conv_gain, conv_taps, attend_gain, feature_weight, value_weight, output_weight, hidden_gain, gate_up, down_weight):

    def one_device(inputs):
        device_index, block_rows, block_edge, slot_rows, slot_edge, slot_live, slot_length, slot_state, slot_keysum = inputs
        group = (device_index % GROUPS).astype(jnp.int32)
        group_state = lax.dynamic_index_in_dim(prefix_state, group, 0, keepdims=False)
        group_keysum = lax.dynamic_index_in_dim(prefix_keysum, group, 0, keepdims=False)
        group_length = lax.dynamic_index_in_dim(prefix_length, group, 0, keepdims=False)
        row_count = block_rows.shape[0]
        normed_block = rounded(root_norm(block_rows, conv_gain))
        series = jnp.concatenate([block_edge.astype(jnp.float32), normed_block], axis=0)
        conv_block = gated_conv(block_rows, normed_block, series[:row_count], series[1:row_count + 1], conv_taps)
        query_rows, key_rows, value_rows = project(conv_block, attend_gain, feature_weight, value_weight)
        local_numer, local_denom = block_local(query_rows, key_rows, value_rows)
        lifted = taylor_features(query_rows.astype(jnp.float32))
        prefix_numer = jnp.einsum('thf,fhv->thv', lifted, group_state.reshape(NF, H, DV), precision=highest)
        prefix_denom = group_length.astype(jnp.float32) + jnp.einsum('thf,fh->th', lifted[..., 1:], group_keysum, precision=highest)
        attended = ((local_numer + rounded(prefix_numer)) / (local_denom + prefix_denom)[..., None]).reshape(row_count, D).astype(jnp.bfloat16)
        block_out = (conv_block.astype(jnp.float32) + jnp.dot(attended, output_weight, preferred_element_type=jnp.float32)).astype(jnp.bfloat16)
        normed_slots = rounded(root_norm(slot_rows, conv_gain))
        conv_slots = gated_conv(slot_rows, normed_slots, slot_edge[:, 0].astype(jnp.float32), slot_edge[:, 1].astype(jnp.float32), conv_taps)
        slot_query, slot_key, slot_value = project(conv_slots, attend_gain, feature_weight, value_weight)
        slot_attended = decode_attend(slot_query, slot_key, slot_value, slot_state, slot_keysum, slot_length)
        slot_out = (conv_slots.astype(jnp.float32) + jnp.dot(slot_attended, output_weight, preferred_element_type=jnp.float32)).astype(jnp.bfloat16)
        joined = jnp.concatenate([block_out, slot_out], axis=0)
        mixed = feed_forward(joined, hidden_gain, gate_up, down_weight)
        slot_mixed = jnp.where(slot_live[:, None] == 1, mixed[row_count:], jnp.zeros_like(mixed[row_count:]))
        return (mixed[:row_count], slot_mixed)
    device_ids = jnp.arange(DEVICES, dtype=jnp.int32)
    prompt_part, decode_part = lax.map(one_device, (device_ids, prompt_rows.reshape(DEVICES, PREFILL, D), prompt_edge, decode_rows.reshape(DEVICES, DEC, D), decode_edge.reshape(DEVICES, DEC, 2, D), decode_live.reshape(DEVICES, DEC), cache_length.reshape(DEVICES, DEC), cache_state.reshape(DEVICES, DEC, NF, D), cache_keysum.reshape(DEVICES, DEC, NF - 1, H)))
    return (prompt_part.reshape(PROMPT_ROWS, D), decode_part.reshape(DECODES, D))
```

```python
import jax
import jax.numpy as jnp
from jax import lax
from jax.experimental import pallas as pl
from jax.experimental.pallas import tpu as pltpu
from jax.sharding import Mesh
from jax.sharding import PartitionSpec as P

D = 1792
H = 16
FD = 16
DV = 112
NF = 273
T = 256
R = 272
MESH = pl.DeviceIdType.MESH

F32 = jnp.float32
BF = jnp.bfloat16
epsilon = 1e-06

ORDERS = (("y", "z", "x"), ("z", "x", "y"), ("x", "y", "z"), ("y", "z"))
GATE, DOWN, UP, PREFIX = range(4)


def dot(a, b):
    return jnp.dot(a, b, preferred_element_type=F32)


def dot_t(a, b):
    return lax.dot_general(a, b, (((1,), (1,)), ((), ())), preferred_element_type=F32)


def norm(values, gain):
    return values * lax.rsqrt(jnp.mean(values * values, axis=-1, keepdims=True) + epsilon) * gain


def iota(shape, dim):
    return lax.broadcasted_iota(jnp.int32, shape, dim)


def layer_kernel(
    rows_ref, edge_ref, slots_ref, slot_two_ref, slot_one_ref, keysum_ref,
    conv_gain_ref, taps_ref, attend_gain_ref, hidden_gain_ref,
    gate_in, down_in, up_in, prefix_in, cache_in, wf_in, wv_in, wo_in,
    out_ref,
    gate, down, up, prefix, wf, wv, wo, cache,
    big, conv, ain, qk, rep, slot_att, pair, tok, attended, hid, give, take, fin,
    local_sem, cache_sem, send_sem, recv_sem, swap_send, swap_recv,
):
    my = {a: lax.axis_index(a) for a in ("z", "y", "x")}
    core = lax.axis_index("c")
    other = 1 - core

    def near(axis, step):
        return lax.rem(my[axis] + (4 + step), 4)

    local = []
    for k, (source, target) in enumerate(((wf_in, wf), (wv_in, wv), (wo_in, wo.at[pl.ds(0, D)]))):
        copy = pltpu.make_async_copy(source, target, local_sem.at[4 + k])
        copy.start()
        local.append(copy)
    cache_copies = []
    for n in range(4):
        cache_copies.append(pltpu.make_async_copy(cache_in.at[n], cache.at[n % 2], cache_sem.at[n]))
    cache_copies[0].start()
    cache_copies[1].start()

    def view(part, sel):
        if part == DOWN:
            z, y = sel["z"], sel["y"]
            if isinstance(z, tuple):
                lanes = pl.ds(pl.multiple_of(y * 512 + z[0] * 128, 128), z[1] * 128)
            else:
                lanes = pl.ds(pl.multiple_of(y * 512 + z * 128, 128), 128)
            x = sel["x"]
            return down.at[pl.ds(*x) if isinstance(x, tuple) else x, :, lanes]
        index = [pl.ds(*sel[a]) if isinstance(sel[a], tuple) else sel[a] for a in ("x", "z", "y")]
        if part == PREFIX:
            return prefix.at[index[1], index[2]]
        return (gate, None, up)[part].at[index[0], index[1], index[2]]

    barrier = pltpu.get_barrier_semaphore()
    for axis in ("z", "y", "x"):
        for step in (1, -1):
            pl.semaphore_signal(barrier, inc=1, device_id={axis: near(axis, step)}, device_id_type=MESH)
    pl.semaphore_signal(barrier, inc=1, device_id={"c": other}, device_id_type=MESH)
    own = []
    for part, source in ((PREFIX, prefix_in), (GATE, gate_in), (DOWN, down_in), (UP, up_in)):
        copy = pltpu.make_async_copy(source, view(part, my), local_sem.at[part])
        copy.start()
        own.append(copy)
    pl.semaphore_wait(barrier, 7)
    for copy in own:
        copy.wait()

    started = []

    def send(part, sel, axis, step, k):
        block = view(part, sel)
        copy = pltpu.make_async_remote_copy(
            block, block, send_sem.at[part, k], recv_sem.at[part, k],
            device_id={axis: near(axis, step)}, device_id_type=MESH)
        copy.start()
        started.append(copy)

    def arrived(part, sel, k):
        block = view(part, sel)
        pltpu.make_async_remote_copy(
            block, block, send_sem.at[part, k], recv_sem.at[part, k],
            device_id={"x": near("x", 1)}, device_id_type=MESH).wait_recv()

    FULL, LOW, HIGH = (0, 4), (0, 2), (2, 2)

    def phase_one(part):
        axis = ORDERS[part][0]
        send(part, my, axis, 1, 0)
        send(part, my, axis, -1, 1)

    def phase_one_on(part):
        axis = ORDERS[part][0]
        sel = {**my, axis: near(axis, -1)}
        arrived(part, sel, 0)
        send(part, sel, axis, 1, 2)

    def phase_one_end(part):
        axis = ORDERS[part][0]
        arrived(part, {**my, axis: near(axis, 1)}, 1)
        arrived(part, {**my, axis: near(axis, 2)}, 2)

    def phase(part, number):
        first, axis = ORDERS[part][0], ORDERS[part][number]
        held = {**my, **{a: FULL for a in ORDERS[part][:number]}}
        k = 3 + 6 * (number - 1)
        send(part, {**held, first: LOW}, axis, 1, k)
        send(part, {**held, first: HIGH}, axis, -1, k + 1)
        send(part, {**held, first: HIGH}, axis, 1, k + 2)
        send(part, {**held, first: LOW}, axis, -1, k + 3)

    def phase_on(part, number):
        first, axis = ORDERS[part][0], ORDERS[part][number]
        held = {**my, **{a: FULL for a in ORDERS[part][:number]}}
        k = 3 + 6 * (number - 1)
        sel = {**held, first: LOW, axis: near(axis, -1)}
        arrived(part, sel, k)
        send(part, sel, axis, 1, k + 4)
        sel = {**held, first: HIGH, axis: near(axis, 1)}
        arrived(part, sel, k + 1)
        send(part, sel, axis, -1, k + 5)

    def phase_near(part, number):
        first, axis = ORDERS[part][0], ORDERS[part][number]
        held = {**my, **{a: FULL for a in ORDERS[part][:number]}}
        k = 3 + 6 * (number - 1)
        arrived(part, {**held, first: HIGH, axis: near(axis, -1)}, k + 2)
        arrived(part, {**held, first: LOW, axis: near(axis, 1)}, k + 3)

    def phase_far(part, number):
        first, axis = ORDERS[part][0], ORDERS[part][number]
        held = {**my, **{a: FULL for a in ORDERS[part][:number]}}
        k = 3 + 6 * (number - 1)
        arrived(part, {**held, first: LOW, axis: near(axis, 2)}, k + 4)
        arrived(part, {**held, first: HIGH, axis: near(axis, 2)}, k + 5)

    everything = (PREFIX, GATE, DOWN, UP)
    for part in everything:
        phase_one(part)

    conv_gain = conv_gain_ref[...]
    big[0:8, 0:D] = edge_ref[...]

    def norm_rows(i, _):
        at = pl.multiple_of(i * 16, 16)
        u = norm(rows_ref[pl.ds(at, 16), :].astype(F32), conv_gain)
        big[pl.ds(pl.multiple_of(at + 8, 8), 16), 0:D] = u.astype(BF).astype(F32)
        return 0

    lax.fori_loop(0, T // 16, norm_rows, 0)
    for part in everything:
        phase_one_on(part)

    def gated(rows, u, one, two):
        convolved = taps_ref[0:1, :] * u + taps_ref[1:2, :] * one + taps_ref[2:3, :] * two
        mixed = (rows.astype(F32) + convolved * jax.nn.sigmoid(u)).astype(BF)
        return mixed, norm(mixed.astype(F32), attend_gain_ref[...]).astype(BF)

    def conv_rows(i, _):
        at = pl.multiple_of(i * 16, 16)
        window = big[pl.ds(at, 24), 0:D]
        mixed, normed = gated(
            rows_ref[pl.ds(at, 16), :], window[8:], pltpu.roll(window, 1, 0)[8:], pltpu.roll(window, 2, 0)[8:])
        conv[pl.ds(at, 16), :] = mixed
        ain[pl.ds(at, 16), :] = normed
        return 0

    lax.fori_loop(0, T // 16, conv_rows, 0)
    slot_u = norm(slots_ref[...].astype(F32), conv_gain).astype(BF).astype(F32)
    mixed, normed = gated(slots_ref[...], slot_u, slot_one_ref[...].astype(F32), slot_two_ref[...].astype(F32))
    conv[T:R, :] = mixed
    ain[T:R, :] = normed

    for part in everything:
        phase_one_end(part)
        phase(part, 1)

    local[0].wait()
    qk[...] = dot(ain[...], wf[...]).astype(BF)
    local[1].wait()

    def value_columns(j, _):
        at = pl.multiple_of(j * 256, 256)
        big[0:R, pl.ds(at, 256)] = dot(ain[...], wv[:, pl.ds(at, 256)]).astype(BF).astype(F32)
        return 0

    lax.fori_loop(0, 3, value_columns, 0)
    for part in everything:
        phase_on(part, 1)
    lax.fori_loop(3, 7, value_columns, 0)

    lane = iota((256, 256), 1)
    feature = iota((256, 256), 0) & 15
    rep[:, 0:256] = (feature == lane >> 4).astype(F32).astype(BF)
    rep[:, 256:512] = (feature == (lane & 15)).astype(F32).astype(BF)

    wide = iota((256, 384), 1)
    deep = iota((256, 384), 0) & 15
    first_sel = jnp.where(wide < 17, wide - 1, (wide - 17) >> 4)
    first_sel = ((deep == first_sel) & (wide < NF)).astype(F32).astype(BF)
    second_sel = ((deep == ((wide - 17) & 15)) & (wide >= 17) & (wide < NF)).astype(F32).astype(BF)
    column = iota((16, 384), 1)
    first_add = (column == 0).astype(F32)
    second_add = jnp.where(column == 0, 1.0, jnp.where(column < 17, FD ** (-0.25), 0.0))
    head_of = (iota((16, 256), 1) >> 4) == iota((16, 256), 0)
    head_start = iota((16, D), 0) * DV
    value_col = iota((16, D), 1)
    head_cols = (value_col >= head_start) & (value_col < head_start + DV)
    slot_qk = qk[T:R, :].astype(F32)
    slot_v = big[T:R, 0:D]
    slot_att[...] = jnp.zeros_like(slot_att)
    for n in range(4):
        cache_copies[n].wait()
        q = jnp.where(head_of, slot_qk[n:n + 1, 0:256], 0.0)
        s = jnp.sum(q * slot_qk[n:n + 1, 256:512], axis=-1, keepdims=True) * FD ** (-0.5)
        weight = 1.0 + s + 0.5 * s * s
        qb = q.astype(BF)
        phi = (dot(qb, first_sel) + first_add) * (dot(qb, second_sel) * (2.0 * FD) ** (-0.5) + second_add)
        den = jnp.sum(phi * keysum_ref[n], axis=-1, keepdims=True) + weight
        phi_high = phi.astype(BF)
        num = dot(phi_high[:, 0:NF], cache[n % 2].astype(BF))
        if n + 2 < 4:
            cache_copies[n + 2].start()
        heads = (num + weight * slot_v[n:n + 1, :]) / den
        slot_att[n:n + 1, 0:D] = jnp.sum(jnp.where(head_cols, heads, 0.0), axis=0, keepdims=True)

    for part in everything:
        phase_near(part, 1)
        phase_far(part, 1)
        if part != PREFIX:
            phase(part, 2)

    for z in range(4):
        for y in range(4):
            h = z * 4 + y
            rep[h * 16:h * 16 + 16, 512:640] = prefix[z, y, 256:272, :]
    big[R:2 * R, 0:D] = jnp.zeros((R, D), F32)
    local[2].wait()
    wo[D:D + 32, :] = jnp.zeros((32, D), BF)
    causal = iota((T, T), 1) <= iota((T, T), 0)
    lane_head = iota((T, 256), 1) >> 4
    lane128 = iota((T, 128), 1)

    def one_head(h):
        qm = jnp.where(lane_head == h, qk[0:T, 0:256].astype(F32), 0.0).astype(BF)
        s = dot_t(qm, qk[0:T, 256:512]) * FD ** (-0.5)
        w = jnp.where(causal, 1.0 + s + 0.5 * s * s, 0.0).astype(BF)
        start = (h * DV // 128) * 128
        window = big[0:T, pl.ds(pl.multiple_of(start, 128), 256)]
        v = pltpu.roll(window, lax.rem(256 + start - h * DV, 256), 1)[:, 0:128]
        v = jnp.where(lane128 < DV, v, jnp.where(lane128 == DV, 1.0, 0.0)).astype(BF)
        phi = (dot(qm, rep[:, 0:256]) * dot(qm, rep[:, 256:512])).astype(BF)
        state = prefix[h // 4, lax.rem(h, 4)]
        num = dot(w, v) + dot(phi, state[0:256]) + dot(qm, rep[:, 512:640]) + state[272:273].astype(F32)
        return jnp.where(lane128 < DV, num / num[:, DV:DV + 1], 0.0)

    lane256 = iota((T, 256), 1)

    def head_pair(p, _):
        left = one_head(2 * p)
        right = one_head(2 * p + 1)
        both = jnp.concatenate([left, jnp.zeros_like(left)], axis=1)
        both = both + pltpu.roll(jnp.concatenate([right, jnp.zeros_like(right)], axis=1), DV, 1)
        pair[0:T, :] = both.astype(BF)
        start = (p * 224 // 128) * 128
        slots = pltpu.roll(slot_att[:, pl.ds(pl.multiple_of(start, 128), 384)], lax.rem(384 + start - p * 224, 384), 1)
        pair[T:R, :] = jnp.where(lane256[0:16] < 224, slots[:, 0:256], 0.0).astype(BF)
        at = pl.multiple_of(p * 224, 32)
        big[R:2 * R, 0:D] += dot(pair[...], wo[pl.ds(at, 256), :])
        return 0

    lax.fori_loop(0, 4, head_pair, 0)
    lax.fori_loop(4, 8, head_pair, 0)

    def hidden_rows(i, _):
        at = pl.multiple_of(i * 16, 16)
        mixed = (conv[pl.ds(at, 16), :].astype(F32) + big[pl.ds(pl.multiple_of(R + at, 16), 16), 0:D]).astype(BF)
        attended[pl.ds(at, 16), :] = mixed
        tok[core, pl.ds(at, 16), :] = norm(mixed.astype(F32), hidden_gain_ref[...]).astype(BF)
        return 0

    lax.fori_loop(0, R // 16, hidden_rows, 0)
    swap = pltpu.make_async_remote_copy(
        tok.at[core], tok.at[core], swap_send.at[0], swap_recv.at[0], device_id={"c": other}, device_id_type=MESH)
    swap.start()
    for part in (GATE, DOWN, UP):
        phase_on(part, 2)
    swap.wait_send()
    pltpu.make_async_remote_copy(
        tok.at[other], tok.at[other], swap_send.at[0], swap_recv.at[0],
        device_id={"c": other}, device_id_type=MESH).wait_recv()
    for part in (GATE, DOWN, UP):
        phase_near(part, 2)
        phase_far(part, 2)

    lane_half = iota((2 * R, 128), 1)

    def feed(x, _):
        tokens = tok[...].reshape(2 * R, D)
        first = dot(tokens, gate[x].reshape(D, 512))
        second = dot(tokens, up[x].reshape(D, 384))
        hid[x, :, 0:384] = (jax.nn.silu(first[:, 0:384]) * second).astype(BF)
        last = first[:, 384:512]
        last = jax.nn.silu(last) * pltpu.roll(last, 64, 1)
        hid[x, :, 384:512] = jnp.where(lane_half < 64, last, 0.0).astype(BF)
        return 0

    lax.fori_loop(0, 4, feed, 0)

    def contract(j, _):
        lanes = pl.ds(pl.multiple_of(j * 256, 256), 256)
        total = dot(hid[0, :, 0:448], down[0, :, lanes])
        for x in range(1, 4):
            total += dot(hid[x, :, 0:448], down[x, :, lanes])
        big[:, lanes] = total
        return 0

    lax.fori_loop(0, 8, contract, 0)

    give[...] = big[pl.ds(pl.multiple_of(other * R, 16), R), :].astype(BF)
    swap = pltpu.make_async_remote_copy(
        give, take, swap_send.at[1], swap_recv.at[1], device_id={"c": other}, device_id_type=MESH)
    swap.start()
    fin[:, 0:D] = attended[...].astype(F32)
    fin[:, D:D + 128] = jnp.zeros((R, 128), F32)
    swap.wait()
    mine = pl.multiple_of(core * R, 16)
    for r in range(H):
        lanes = ((r % 4) * 4 + r // 4) * 128
        piece = big[pl.ds(mine, R), lanes:lanes + 128] + take[:, lanes:lanes + 128].astype(F32)
        start = r * DV // 128 * 128
        piece = pltpu.roll(jnp.concatenate([piece, jnp.zeros_like(piece)], axis=1), r * DV - start, 1)
        fin[:, start:start + 256] += piece
    out_ref[...] = fin[:, 0:D].astype(BF)
    for copy in started:
        copy.wait_send()


def on_device(
    prompt_rows, prompt_edge, decode_rows, decode_edge, decode_live, cache_length, cache_state,
    cache_keysum, prefix_length, prefix_state, prefix_keysum, conv_gain, conv_taps, attend_gain,
    feature_weight, value_weight, output_weight, hidden_gain, gate_up, down_weight,
):
    gate_in = jnp.concatenate([gate_up[0], gate_up[1, :, 384:]], axis=1)
    up_in = gate_up[1, :, :384]
    down_in = jnp.pad(down_weight, ((0, 0), (0, 16)))
    sums = jnp.concatenate([prefix_length.astype(F32)[:, None], prefix_keysum[0]], axis=0)
    state = jnp.concatenate([prefix_state[0], sums, jnp.zeros((NF, 15), F32)], axis=1)
    prefix_in = jnp.concatenate([
        state[17:] * (2.0 * FD) ** (-0.5), state[1:17] * FD ** (-0.25), state[0:1], jnp.zeros((15, 128), F32)],
        axis=0).astype(BF)
    lengths = jnp.broadcast_to(cache_length.astype(F32)[:, None, None], (4, H, 1))
    keysum = jnp.concatenate(
        [lengths, jnp.transpose(cache_keysum, (0, 2, 1)), jnp.zeros((4, H, 384 - NF), F32)], axis=2)
    edge = jnp.pad(prompt_edge[0].astype(F32), ((6, 0), (0, 0)))
    spare = ((0, 12), (0, 0))
    vmem = pl.BlockSpec(memory_space=pltpu.VMEM)
    hbm = pl.BlockSpec(memory_space=pl.ANY)
    out = pl.pallas_call(
        layer_kernel,
        out_shape=jax.ShapeDtypeStruct((R, D), BF),
        in_specs=[vmem] * 10 + [hbm] * 8,
        out_specs=vmem,
        scratch_shapes=[
            pltpu.VMEM((4, 4, 4, 112, 512), BF),
            pltpu.VMEM((4, 448, 2048), BF),
            pltpu.VMEM((4, 4, 4, 112, 384), BF),
            pltpu.VMEM((4, 4, 288, 128), BF),
            pltpu.VMEM((D, 512), BF),
            pltpu.VMEM((D, D), BF),
            pltpu.VMEM((D + 32, D), BF),
            pltpu.VMEM((2, NF, D), F32),
            pltpu.VMEM((2 * R, 2048), F32),
            pltpu.VMEM((R, D), BF),
            pltpu.VMEM((R, D), BF),
            pltpu.VMEM((R, 512), BF),
            pltpu.VMEM((256, 640), BF),
            pltpu.VMEM((16, 2048), F32),
            pltpu.VMEM((R, 256), BF),
            pltpu.VMEM((2, R, D), BF),
            pltpu.VMEM((R, D), BF),
            pltpu.VMEM((4, 2 * R, 512), BF),
            pltpu.VMEM((R, 2048), BF),
            pltpu.VMEM((R, 2048), BF),
            pltpu.VMEM((R, D + 128), F32),
            pltpu.SemaphoreType.DMA((7,)),
            pltpu.SemaphoreType.DMA((4,)),
            pltpu.SemaphoreType.DMA((4, 15)),
            pltpu.SemaphoreType.DMA((4, 15)),
            pltpu.SemaphoreType.DMA((2,)),
            pltpu.SemaphoreType.DMA((2,)),
        ],
        compiler_params=pltpu.CompilerParams(
            collective_id=0, has_side_effects=True, vmem_limit_bytes=67043328),
    )(
        prompt_rows, edge, jnp.pad(decode_rows, spare), jnp.pad(decode_edge[:, 0], spare),
        jnp.pad(decode_edge[:, 1], spare), keysum, conv_gain[None], conv_taps, attend_gain[None],
        hidden_gain[None], gate_in, down_in, up_in, prefix_in, cache_state, feature_weight,
        value_weight, output_weight,
    )
    slots = out[T:T + 4]
    return out[:T], jnp.where(decode_live[:, None] == 1, slots, jnp.zeros_like(slots))


def solution(mesh):
    torus = Mesh(mesh.devices.reshape(4, 4, 4, 2), ("z", "y", "x", "c"))
    rows, req, mlp = ("z", "y", "x", "c"), ("z", "y"), ("x", "c")
    return jax.shard_map(
        on_device,
        mesh=torus,
        in_specs=(
            P(rows, None), P(rows, None, None), P(rows, None), P(rows, None, None), P(rows), P(rows),
            P(rows, None, None), P(rows, None, None), P(mlp), P(mlp, None, req), P(mlp, None, req),
            P(), P(), P(), P(), P(), P(), P(), P(None, req, mlp), P(mlp, req),
        ),
        out_specs=(P(rows, None), P(rows, None)),
        check_vma=False,
    )
```

```python
import jax
import jax.numpy as jnp
from jax import lax
from jax.experimental import pallas as pl
from jax.experimental.pallas import tpu as pltpu
from jax.sharding import Mesh
from jax.sharding import PartitionSpec as P

D = 1792
H = 16
FD = 16
DV = 112
NF = 273
T = 256
R = 272
MESH = pl.DeviceIdType.MESH

F32 = jnp.float32
BF = jnp.bfloat16
epsilon = 1e-06

ORDERS = (("y", "z", "x"), ("z", "x", "y"), ("x", "y", "z"), ("y", "z"))
GATE, DOWN, UP, PREFIX = range(4)


def dot(a, b):
    return jnp.dot(a, b, preferred_element_type=F32)


def dot_t(a, b):
    return lax.dot_general(a, b, (((1,), (1,)), ((), ())), preferred_element_type=F32)


def norm(values, gain):
    return values * lax.rsqrt(jnp.mean(values * values, axis=-1, keepdims=True) + epsilon) * gain


def iota(shape, dim):
    return lax.broadcasted_iota(jnp.int32, shape, dim)


def layer_kernel(
    rows_ref, edge_ref, slots_ref, slot_edge_ref, keysum_ref, gains_ref, taps_ref,
    prefix_state_ref, prefix_keys_ref, prefix_length_ref, length_ref, live_ref,
    feed_in, down_in, cache_in, wf_in, wv_in, wo_in,
    out_ref, slot_out_ref,
    gate, down, up, prefix, wf, wv, wo, cache,
    big, conv, ain, qk, rep, slot_att, pair, tok, attended, hid, give, take, fin, slot_rows,
    local_sem, cache_sem, send_sem, recv_sem, swap_send, swap_recv,
):
    my = {a: lax.axis_index(a) for a in ("z", "y", "x")}
    core = lax.axis_index("c")
    other = 1 - core

    def near(axis, step):
        return lax.rem(my[axis] + (4 + step), 4)

    local = []
    for k, (source, target) in enumerate(((wf_in, wf), (wv_in, wv), (wo_in, wo.at[pl.ds(0, D)]))):
        copy = pltpu.make_async_copy(source, target, local_sem.at[4 + k])
        copy.start()
        local.append(copy)
    cache_copies = []
    for n in range(4):
        cache_copies.append(pltpu.make_async_copy(cache_in.at[:, n], cache.at[n % 2], cache_sem.at[n]))
    cache_copies[0].start()
    cache_copies[1].start()

    def view(part, sel):
        if part == DOWN:
            z, y = sel["z"], sel["y"]
            if isinstance(z, tuple):
                lanes = pl.ds(pl.multiple_of(y * 512 + z[0] * 128, 128), z[1] * 128)
            else:
                lanes = pl.ds(pl.multiple_of(y * 512 + z * 128, 128), 128)
            x = sel["x"]
            return down.at[pl.ds(*x) if isinstance(x, tuple) else x, :, lanes]
        index = [pl.ds(*sel[a]) if isinstance(sel[a], tuple) else sel[a] for a in ("x", "z", "y")]
        if part == PREFIX:
            return prefix.at[index[1], index[2]]
        return (gate, None, up)[part].at[index[0], index[1], index[2]]

    barrier = pltpu.get_barrier_semaphore()
    for axis in ("z", "y", "x"):
        for step in (1, -1):
            pl.semaphore_signal(barrier, inc=1, device_id={axis: near(axis, step)}, device_id_type=MESH)
    pl.semaphore_signal(barrier, inc=1, device_id={"c": other}, device_id_type=MESH)
    own = []
    for part, source in (
        (GATE, feed_in.at[:, pl.ds(0, 512)]), (DOWN, down_in), (UP, feed_in.at[:, pl.ds(512, 384)])):
        copy = pltpu.make_async_copy(source, view(part, my), local_sem.at[part])
        copy.start()
        own.append(copy)

    key_column = jnp.sum(
        jnp.where(iota((NF - 1, NF - 1), 0) == iota((NF - 1, NF - 1), 1), prefix_keys_ref[...], 0.0),
        axis=1, keepdims=True)
    own_prefix = prefix.at[my["z"], my["y"]]
    square = jnp.where(iota((256, 128), 1) == DV, key_column[16:272], prefix_state_ref[17:273, :])
    own_prefix[0:256, :] = (square * (2.0 * FD) ** (-0.5)).astype(BF)
    linear = jnp.where(iota((16, 128), 1) == DV, key_column[0:16], prefix_state_ref[1:17, :])
    own_prefix[256:272, :] = (linear * FD ** (-0.25)).astype(BF)
    constant = jnp.where(
        iota((16, 128), 1) == DV, prefix_length_ref[0].astype(F32), prefix_state_ref[0:1, :])
    own_prefix[272:288, :] = jnp.where(iota((16, 128), 0) == 0, constant, 0.0).astype(BF)
    pl.semaphore_wait(barrier, 7)
    for copy in own:
        copy.wait()

    started = []

    def send(part, sel, axis, step, k):
        block = view(part, sel)
        copy = pltpu.make_async_remote_copy(
            block, block, send_sem.at[part, k], recv_sem.at[part, k],
            device_id={axis: near(axis, step)}, device_id_type=MESH)
        copy.start()
        started.append(copy)

    def arrived(part, sel, k):
        block = view(part, sel)
        pltpu.make_async_remote_copy(
            block, block, send_sem.at[part, k], recv_sem.at[part, k],
            device_id={"x": near("x", 1)}, device_id_type=MESH).wait_recv()

    FULL, LOW, HIGH = (0, 4), (0, 2), (2, 2)

    def phase_one(part):
        axis = ORDERS[part][0]
        send(part, my, axis, 1, 0)
        send(part, my, axis, -1, 1)

    def phase_one_on(part):
        axis = ORDERS[part][0]
        sel = {**my, axis: near(axis, -1)}
        arrived(part, sel, 0)
        send(part, sel, axis, 1, 2)

    def phase_one_end(part):
        axis = ORDERS[part][0]
        arrived(part, {**my, axis: near(axis, 1)}, 1)
        arrived(part, {**my, axis: near(axis, 2)}, 2)

    def phase(part, number):
        first, axis = ORDERS[part][0], ORDERS[part][number]
        held = {**my, **{a: FULL for a in ORDERS[part][:number]}}
        k = 3 + 6 * (number - 1)
        send(part, {**held, first: LOW}, axis, 1, k)
        send(part, {**held, first: HIGH}, axis, -1, k + 1)
        send(part, {**held, first: HIGH}, axis, 1, k + 2)
        send(part, {**held, first: LOW}, axis, -1, k + 3)

    def phase_on(part, number):
        first, axis = ORDERS[part][0], ORDERS[part][number]
        held = {**my, **{a: FULL for a in ORDERS[part][:number]}}
        k = 3 + 6 * (number - 1)
        sel = {**held, first: LOW, axis: near(axis, -1)}
        arrived(part, sel, k)
        send(part, sel, axis, 1, k + 4)
        sel = {**held, first: HIGH, axis: near(axis, 1)}
        arrived(part, sel, k + 1)
        send(part, sel, axis, -1, k + 5)

    def phase_near(part, number):
        first, axis = ORDERS[part][0], ORDERS[part][number]
        held = {**my, **{a: FULL for a in ORDERS[part][:number]}}
        k = 3 + 6 * (number - 1)
        arrived(part, {**held, first: HIGH, axis: near(axis, -1)}, k + 2)
        arrived(part, {**held, first: LOW, axis: near(axis, 1)}, k + 3)

    def phase_far(part, number):
        first, axis = ORDERS[part][0], ORDERS[part][number]
        held = {**my, **{a: FULL for a in ORDERS[part][:number]}}
        k = 3 + 6 * (number - 1)
        arrived(part, {**held, first: LOW, axis: near(axis, 2)}, k + 4)
        arrived(part, {**held, first: HIGH, axis: near(axis, 2)}, k + 5)

    everything = (PREFIX, GATE, DOWN, UP)
    for part in everything:
        phase_one(part)

    conv_gain = gains_ref[0:1, :]
    big[0:8, 0:D] = jnp.zeros((8, D), F32)
    big[6:8, 0:D] = edge_ref[...].astype(F32)

    def norm_rows(i, _):
        at = pl.multiple_of(i * 16, 16)
        u = norm(rows_ref[pl.ds(at, 16), :].astype(F32), conv_gain)
        big[pl.ds(pl.multiple_of(at + 8, 8), 16), 0:D] = u.astype(BF).astype(F32)
        return 0

    lax.fori_loop(0, T // 16, norm_rows, 0)
    for part in everything:
        phase_one_on(part)

    def gated(rows, u, one, two):
        convolved = taps_ref[0:1, :] * u + taps_ref[1:2, :] * one + taps_ref[2:3, :] * two
        mixed = (rows.astype(F32) + convolved * jax.nn.sigmoid(u)).astype(BF)
        return mixed, norm(mixed.astype(F32), gains_ref[1:2, :]).astype(BF)

    def conv_rows(i, _):
        at = pl.multiple_of(i * 16, 16)
        window = big[pl.ds(at, 24), 0:D]
        mixed, normed = gated(
            rows_ref[pl.ds(at, 16), :], window[8:], pltpu.roll(window, 1, 0)[8:], pltpu.roll(window, 2, 0)[8:])
        conv[pl.ds(at, 16), :] = mixed
        ain[pl.ds(at, 16), :] = normed
        return 0

    lax.fori_loop(0, T // 16, conv_rows, 0)
    slot_rows[...] = jnp.zeros_like(slot_rows)
    slot_rows[0, 0:4, :] = slots_ref[...].astype(F32)
    for n in range(4):
        before = slot_edge_ref[n].astype(F32)
        slot_rows[2, n:n + 1, :] = before[0:1]
        slot_rows[1, n:n + 1, :] = before[1:2]
    slot_u = norm(slot_rows[0], conv_gain).astype(BF).astype(F32)
    mixed, normed = gated(slot_rows[0], slot_u, slot_rows[1], slot_rows[2])
    conv[T:R, :] = mixed
    ain[T:R, :] = normed

    for part in everything:
        phase_one_end(part)
        phase(part, 1)

    local[0].wait()
    qk[...] = dot(ain[...], wf[...]).astype(BF)
    local[1].wait()

    def value_columns(j, _):
        at = pl.multiple_of(j * 256, 256)
        big[0:R, pl.ds(at, 256)] = dot(ain[...], wv[:, pl.ds(at, 256)]).astype(BF).astype(F32)
        return 0

    lax.fori_loop(0, 3, value_columns, 0)
    for part in everything:
        phase_on(part, 1)
    lax.fori_loop(3, 7, value_columns, 0)

    lane = iota((256, 256), 1)
    feature = iota((256, 256), 0) & 15
    rep[:, 0:256] = (feature == lane >> 4).astype(F32).astype(BF)
    rep[:, 256:512] = (feature == (lane & 15)).astype(F32).astype(BF)

    wide = iota((256, 384), 1)
    deep = iota((256, 384), 0) & 15
    first_sel = jnp.where(wide < 17, wide - 1, (wide - 17) >> 4)
    first_sel = ((deep == first_sel) & (wide < NF)).astype(F32).astype(BF)
    second_sel = ((deep == ((wide - 17) & 15)) & (wide >= 17) & (wide < NF)).astype(F32).astype(BF)
    column = iota((16, 384), 1)
    first_add = (column == 0).astype(F32)
    second_add = jnp.where(column == 0, 1.0, jnp.where(column < 17, FD ** (-0.25), 0.0))
    head_of = (iota((16, 256), 1) >> 4) == iota((16, 256), 0)
    head_start = iota((16, D), 0) * DV
    value_col = iota((16, D), 1)
    head_cols = (value_col >= head_start) & (value_col < head_start + DV)
    slot_qk = qk[T:R, :].astype(F32)
    slot_v = big[T:R, 0:D]
    slot_att[...] = jnp.zeros_like(slot_att)
    for n in range(4):
        cache_copies[n].wait()
        q = jnp.where(head_of, slot_qk[n:n + 1, 0:256], 0.0)
        s = jnp.sum(q * slot_qk[n:n + 1, 256:512], axis=-1, keepdims=True) * FD ** (-0.5)
        weight = 1.0 + s + 0.5 * s * s
        qb = q.astype(BF)
        phi = (dot(qb, first_sel) + first_add) * (dot(qb, second_sel) * (2.0 * FD) ** (-0.5) + second_add)
        rest = jnp.where(column == 0, 0.0, phi)[:, 0:NF]
        sums = pltpu.roll(keysum_ref[n], 1, 1)[:, 0:NF]
        den = jnp.sum(rest * sums, axis=-1, keepdims=True) + length_ref[n].astype(F32) + weight
        phi_high = phi.astype(BF)
        num = dot(phi_high[:, 0:NF], cache[n % 2].astype(BF))
        if n + 2 < 4:
            cache_copies[n + 2].start()
        heads = (num + weight * slot_v[n:n + 1, :]) / den
        slot_att[n:n + 1, 0:D] = jnp.sum(jnp.where(head_cols, heads, 0.0), axis=0, keepdims=True)

    for part in everything:
        phase_near(part, 1)
        phase_far(part, 1)
        if part != PREFIX:
            phase(part, 2)

    for z in range(4):
        for y in range(4):
            h = z * 4 + y
            rep[h * 16:h * 16 + 16, 512:640] = prefix[z, y, 256:272, :]
    big[R:2 * R, 0:D] = jnp.zeros((R, D), F32)
    local[2].wait()
    wo[D:D + 32, :] = jnp.zeros((32, D), BF)
    causal = iota((T, T), 1) <= iota((T, T), 0)
    lane_head = iota((T, 256), 1) >> 4
    lane128 = iota((T, 128), 1)

    def one_head(h):
        qm = jnp.where(lane_head == h, qk[0:T, 0:256].astype(F32), 0.0).astype(BF)
        s = dot_t(qm, qk[0:T, 256:512]) * FD ** (-0.5)
        w = jnp.where(causal, 1.0 + s + 0.5 * s * s, 0.0).astype(BF)
        start = (h * DV // 128) * 128
        window = big[0:T, pl.ds(pl.multiple_of(start, 128), 256)]
        v = pltpu.roll(window, lax.rem(256 + start - h * DV, 256), 1)[:, 0:128]
        v = jnp.where(lane128 < DV, v, jnp.where(lane128 == DV, 1.0, 0.0)).astype(BF)
        phi = (dot(qm, rep[:, 0:256]) * dot(qm, rep[:, 256:512])).astype(BF)
        state = prefix[h // 4, lax.rem(h, 4)]
        num = dot(w, v) + dot(phi, state[0:256]) + dot(qm, rep[:, 512:640]) + state[272:273].astype(F32)
        return jnp.where(lane128 < DV, num / num[:, DV:DV + 1], 0.0)

    lane256 = iota((T, 256), 1)

    def head_pair(p, _):
        left = one_head(2 * p)
        right = one_head(2 * p + 1)
        both = jnp.concatenate([left, jnp.zeros_like(left)], axis=1)
        both = both + pltpu.roll(jnp.concatenate([right, jnp.zeros_like(right)], axis=1), DV, 1)
        pair[0:T, :] = both.astype(BF)
        start = (p * 224 // 128) * 128
        slots = pltpu.roll(slot_att[:, pl.ds(pl.multiple_of(start, 128), 384)], lax.rem(384 + start - p * 224, 384), 1)
        pair[T:R, :] = jnp.where(lane256[0:16] < 224, slots[:, 0:256], 0.0).astype(BF)
        at = pl.multiple_of(p * 224, 32)
        big[R:2 * R, 0:D] += dot(pair[...], wo[pl.ds(at, 256), :])
        return 0

    lax.fori_loop(0, 4, head_pair, 0)
    lax.fori_loop(4, 8, head_pair, 0)

    def hidden_rows(i, _):
        at = pl.multiple_of(i * 16, 16)
        mixed = (conv[pl.ds(at, 16), :].astype(F32) + big[pl.ds(pl.multiple_of(R + at, 16), 16), 0:D]).astype(BF)
        attended[pl.ds(at, 16), :] = mixed
        tok[core, pl.ds(at, 16), :] = norm(mixed.astype(F32), gains_ref[2:3, :]).astype(BF)
        return 0

    lax.fori_loop(0, R // 16, hidden_rows, 0)
    swap = pltpu.make_async_remote_copy(
        tok.at[core], tok.at[core], swap_send.at[0], swap_recv.at[0], device_id={"c": other}, device_id_type=MESH)
    swap.start()
    for part in (GATE, DOWN, UP):
        phase_on(part, 2)
    swap.wait_send()
    pltpu.make_async_remote_copy(
        tok.at[other], tok.at[other], swap_send.at[0], swap_recv.at[0],
        device_id={"c": other}, device_id_type=MESH).wait_recv()
    for part in (GATE, DOWN, UP):
        phase_near(part, 2)
        phase_far(part, 2)

    lane_half = iota((2 * R, 128), 1)

    def feed(x, _):
        tokens = tok[...].reshape(2 * R, D)
        first = dot(tokens, gate[x].reshape(D, 512))
        second = dot(tokens, up[x].reshape(D, 384))
        hid[x, :, 0:384] = (jax.nn.silu(first[:, 0:384]) * second).astype(BF)
        last = first[:, 384:512]
        last = jax.nn.silu(last) * pltpu.roll(last, 64, 1)
        hid[x, :, 384:512] = jnp.where(lane_half < 64, last, 0.0).astype(BF)
        return 0

    lax.fori_loop(0, 4, feed, 0)

    def contract(j, _):
        lanes = pl.ds(pl.multiple_of(j * 256, 256), 256)
        total = dot(hid[0, :, 0:448], down[0, :, lanes])
        for x in range(1, 4):
            total += dot(hid[x, :, 0:448], down[x, :, lanes])
        big[:, lanes] = total
        return 0

    lax.fori_loop(0, 8, contract, 0)

    give[...] = big[pl.ds(pl.multiple_of(other * R, 16), R), :].astype(BF)
    swap = pltpu.make_async_remote_copy(
        give, take, swap_send.at[1], swap_recv.at[1], device_id={"c": other}, device_id_type=MESH)
    swap.start()
    fin[:, 0:D] = attended[...].astype(F32)
    fin[:, D:D + 128] = jnp.zeros((R, 128), F32)
    swap.wait()
    mine = pl.multiple_of(core * R, 16)
    for r in range(H):
        lanes = ((r % 4) * 4 + r // 4) * 128
        piece = big[pl.ds(mine, R), lanes:lanes + 128] + take[:, lanes:lanes + 128].astype(F32)
        start = r * DV // 128 * 128
        piece = pltpu.roll(jnp.concatenate([piece, jnp.zeros_like(piece)], axis=1), r * DV - start, 1)
        fin[:, start:start + 256] += piece
    out_ref[...] = fin[0:T, 0:D].astype(BF)
    live = iota((4, D), 0)
    for n in range(4):
        live = jnp.where(iota((4, D), 0) == n, live_ref[n], live)
    slot_out_ref[...] = jnp.where(live == 1, fin[T:T + 4, 0:D], 0.0).astype(BF)
    for copy in started:
        copy.wait_send()


def on_device(
    prompt_rows, prompt_edge, decode_rows, decode_edge, decode_live, cache_length, cache_state,
    cache_keysum, prefix_length, prefix_state, prefix_keysum, conv_gain, conv_taps, attend_gain,
    feature_weight, value_weight, output_weight, hidden_gain, gate_up, down_weight,
):
    feed_in = jnp.concatenate([gate_up[0], gate_up[1, :, 384:], gate_up[1, :, :384]], axis=1)
    down_in = jnp.pad(down_weight, ((0, 0), (0, 16)))
    state_in = jnp.pad(prefix_state[0], ((0, 15), (0, 16)))
    keysum = jnp.pad(jnp.transpose(cache_keysum, (0, 2, 1)), ((0, 0), (0, 0), (0, 112)))
    gains = jnp.stack([conv_gain, attend_gain, hidden_gain])
    vmem = pl.BlockSpec(memory_space=pltpu.VMEM)
    smem = pl.BlockSpec(memory_space=pltpu.SMEM)
    hbm = pl.BlockSpec(memory_space=pl.ANY)
    return pl.pallas_call(
        layer_kernel,
        out_shape=(jax.ShapeDtypeStruct((T, D), BF), jax.ShapeDtypeStruct((4, D), BF)),
        in_specs=[vmem] * 9 + [smem] * 3 + [hbm] * 6,
        out_specs=(vmem, vmem),
        scratch_shapes=[
            pltpu.VMEM((4, 4, 4, 112, 512), BF),
            pltpu.VMEM((4, 448, 2048), BF),
            pltpu.VMEM((4, 4, 4, 112, 384), BF),
            pltpu.VMEM((4, 4, 288, 128), BF),
            pltpu.VMEM((D, 512), BF),
            pltpu.VMEM((D, D), BF),
            pltpu.VMEM((D + 32, D), BF),
            pltpu.VMEM((2, NF, D), F32),
            pltpu.VMEM((2 * R, 2048), F32),
            pltpu.VMEM((R, D), BF),
            pltpu.VMEM((R, D), BF),
            pltpu.VMEM((R, 512), BF),
            pltpu.VMEM((256, 640), BF),
            pltpu.VMEM((16, 2048), F32),
            pltpu.VMEM((R, 256), BF),
            pltpu.VMEM((2, R, D), BF),
            pltpu.VMEM((R, D), BF),
            pltpu.VMEM((4, 2 * R, 512), BF),
            pltpu.VMEM((R, 2048), BF),
            pltpu.VMEM((R, 2048), BF),
            pltpu.VMEM((R, D + 128), F32),
            pltpu.VMEM((3, 16, D), F32),
            pltpu.SemaphoreType.DMA((7,)),
            pltpu.SemaphoreType.DMA((4,)),
            pltpu.SemaphoreType.DMA((4, 15)),
            pltpu.SemaphoreType.DMA((4, 15)),
            pltpu.SemaphoreType.DMA((2,)),
            pltpu.SemaphoreType.DMA((2,)),
        ],
        compiler_params=pltpu.CompilerParams(
            collective_id=0, has_side_effects=True, vmem_limit_bytes=67043328),
    )(
        prompt_rows, prompt_edge[0], decode_rows, decode_edge, keysum, gains, conv_taps,
        state_in, jnp.transpose(prefix_keysum[0]), prefix_length, cache_length, decode_live,
        feed_in, down_in, jnp.transpose(cache_state, (1, 0, 2)), feature_weight, value_weight,
        output_weight,
    )


def solution(mesh):
    torus = Mesh(mesh.devices.reshape(4, 4, 4, 2), ("z", "y", "x", "c"))
    rows, req, mlp = ("z", "y", "x", "c"), ("z", "y"), ("x", "c")
    return jax.shard_map(
        on_device,
        mesh=torus,
        in_specs=(
            P(rows, None), P(rows, None, None), P(rows, None), P(rows, None, None), P(rows), P(rows),
            P(rows, None, None), P(rows, None, None), P(mlp), P(mlp, None, req), P(mlp, None, req),
            P(), P(), P(), P(), P(), P(), P(), P(None, req, mlp), P(mlp, req),
        ),
        out_specs=(P(rows, None), P(rows, None)),
        check_vma=False,
    )
```

```python
import jax
import jax.numpy as jnp
from jax import lax
from jax.experimental import pallas as pl
from jax.experimental.pallas import tpu as pltpu
from jax.sharding import Mesh
from jax.sharding import PartitionSpec as P

D = 1792
H = 16
FD = 16
DV = 112
NF = 273
T = 256
R = 272
MESH = pl.DeviceIdType.MESH

F32 = jnp.float32
BF = jnp.bfloat16
epsilon = 1e-06

ORDERS = (("y", "z", "x"), ("z", "x", "y"), ("x", "y", "z"), ("y", "z"))
GATE, DOWN, UP, PREFIX = range(4)


def dot(a, b):
    return jnp.dot(a, b, preferred_element_type=F32)


def dot_t(a, b):
    return lax.dot_general(a, b, (((1,), (1,)), ((), ())), preferred_element_type=F32)


def norm(values, gain):
    return values * lax.rsqrt(jnp.mean(values * values, axis=-1, keepdims=True) + epsilon) * gain


def iota(shape, dim):
    return lax.broadcasted_iota(jnp.int32, shape, dim)


def layer_kernel(
    rows_ref, edge_ref, slots_ref, slot_edge_ref, keysum_ref, gains_ref, taps_ref,
    prefix_state_ref, prefix_keys_ref, prefix_length_ref, length_ref, live_ref,
    gate_up_ref, down_ref, cache_in, wf_in, wv_in, wo_in,
    out_ref, slot_out_ref,
    gate, down, up, prefix, wf, wv, wo, cache,
    big, conv, ain, qk, rep, slot_att, pair, tok, attended, hid, give, take, fin, slot_rows, stage, sums_row,
    local_sem, cache_sem, send_sem, recv_sem, swap_send, swap_recv,
):
    my = {a: lax.axis_index(a) for a in ("z", "y", "x")}
    core = lax.axis_index("c")
    other = 1 - core

    def near(axis, step):
        return lax.rem(my[axis] + (4 + step), 4)

    local = []
    for k, (source, target) in enumerate(((wf_in, wf), (wv_in, wv), (wo_in, wo.at[pl.ds(0, D)]))):
        copy = pltpu.make_async_copy(source, target, local_sem.at[k])
        copy.start()
        local.append(copy)
    cache_copies = []
    for n in range(4):
        cache_copies.append(pltpu.make_async_copy(cache_in.at[:, n], cache.at[n % 2], cache_sem.at[n]))
    cache_copies[0].start()
    cache_copies[1].start()

    def view(part, sel):
        if part == DOWN:
            z, y = sel["z"], sel["y"]
            if isinstance(z, tuple):
                lanes = pl.ds(pl.multiple_of(y * 512 + z[0] * 128, 128), z[1] * 128)
            else:
                lanes = pl.ds(pl.multiple_of(y * 512 + z * 128, 128), 128)
            x = sel["x"]
            return down.at[pl.ds(*x) if isinstance(x, tuple) else x, :, lanes]
        index = [pl.ds(*sel[a]) if isinstance(sel[a], tuple) else sel[a] for a in ("x", "z", "y")]
        if part == PREFIX:
            return prefix.at[index[1], index[2]]
        return (gate, None, up)[part].at[index[0], index[1], index[2]]

    barrier = pltpu.get_barrier_semaphore()
    for axis in ("z", "y", "x"):
        for step in (1, -1):
            pl.semaphore_signal(barrier, inc=1, device_id={axis: near(axis, step)}, device_id_type=MESH)
    pl.semaphore_signal(barrier, inc=1, device_id={"c": other}, device_id_type=MESH)
    own_gate = gate.at[my["x"], my["z"], my["y"]]
    own_gate[:, 0:384] = gate_up_ref[0, :, 0:384]
    stage[0:112, 0:64] = gate_up_ref[0, :, 384:448].astype(F32)
    stage[112:224, 0:64] = gate_up_ref[1, :, 384:448].astype(F32)
    tail = jnp.where(iota((112, 128), 1) < 64, stage[0:112, :], pltpu.roll(stage[112:224, :], 64, 1))
    own_gate[:, 384:512] = tail.astype(BF)
    up[my["x"], my["z"], my["y"]] = gate_up_ref[1, :, 0:384]
    stage[:, 0:DV] = down_ref[...].astype(F32)
    own_lanes = pl.ds(pl.multiple_of(my["y"] * 512 + my["z"] * 128, 128), 128)
    down[my["x"], :, own_lanes] = jnp.where(iota((448, 128), 1) < DV, stage[...], 0.0).astype(BF)
    key_column = jnp.sum(
        jnp.where(iota((NF - 1, NF - 1), 0) == iota((NF - 1, NF - 1), 1), prefix_keys_ref[...], 0.0),
        axis=1, keepdims=True)
    own_prefix = prefix.at[my["z"], my["y"]]
    square = jnp.where(iota((256, 128), 1) == DV, key_column[16:272], prefix_state_ref[17:273, :])
    own_prefix[0:256, :] = (square * (2.0 * FD) ** (-0.5)).astype(BF)
    linear = jnp.where(iota((16, 128), 1) == DV, key_column[0:16], prefix_state_ref[1:17, :])
    own_prefix[256:272, :] = (linear * FD ** (-0.25)).astype(BF)
    constant = jnp.where(
        iota((16, 128), 1) == DV, prefix_length_ref[0].astype(F32), prefix_state_ref[0:1, :])
    own_prefix[272:288, :] = jnp.where(iota((16, 128), 0) == 0, constant, 0.0).astype(BF)
    pl.semaphore_wait(barrier, 7)

    started = []

    def send(part, sel, axis, step, k):
        block = view(part, sel)
        copy = pltpu.make_async_remote_copy(
            block, block, send_sem.at[part, k], recv_sem.at[part, k],
            device_id={axis: near(axis, step)}, device_id_type=MESH)
        copy.start()
        started.append(copy)

    def arrived(part, sel, k):
        block = view(part, sel)
        pltpu.make_async_remote_copy(
            block, block, send_sem.at[part, k], recv_sem.at[part, k],
            device_id={"x": near("x", 1)}, device_id_type=MESH).wait_recv()

    FULL, LOW, HIGH = (0, 4), (0, 2), (2, 2)

    def phase_one(part):
        axis = ORDERS[part][0]
        send(part, my, axis, 1, 0)
        send(part, my, axis, -1, 1)

    def phase_one_on(part):
        axis = ORDERS[part][0]
        sel = {**my, axis: near(axis, -1)}
        arrived(part, sel, 0)
        send(part, sel, axis, 1, 2)

    def phase_one_end(part):
        axis = ORDERS[part][0]
        arrived(part, {**my, axis: near(axis, 1)}, 1)
        arrived(part, {**my, axis: near(axis, 2)}, 2)

    def phase(part, number):
        first, axis = ORDERS[part][0], ORDERS[part][number]
        held = {**my, **{a: FULL for a in ORDERS[part][:number]}}
        k = 3 + 6 * (number - 1)
        send(part, {**held, first: LOW}, axis, 1, k)
        send(part, {**held, first: HIGH}, axis, -1, k + 1)
        send(part, {**held, first: HIGH}, axis, 1, k + 2)
        send(part, {**held, first: LOW}, axis, -1, k + 3)

    def phase_on(part, number):
        first, axis = ORDERS[part][0], ORDERS[part][number]
        held = {**my, **{a: FULL for a in ORDERS[part][:number]}}
        k = 3 + 6 * (number - 1)
        sel = {**held, first: LOW, axis: near(axis, -1)}
        arrived(part, sel, k)
        send(part, sel, axis, 1, k + 4)
        sel = {**held, first: HIGH, axis: near(axis, 1)}
        arrived(part, sel, k + 1)
        send(part, sel, axis, -1, k + 5)

    def phase_near(part, number):
        first, axis = ORDERS[part][0], ORDERS[part][number]
        held = {**my, **{a: FULL for a in ORDERS[part][:number]}}
        k = 3 + 6 * (number - 1)
        arrived(part, {**held, first: HIGH, axis: near(axis, -1)}, k + 2)
        arrived(part, {**held, first: LOW, axis: near(axis, 1)}, k + 3)

    def phase_far(part, number):
        first, axis = ORDERS[part][0], ORDERS[part][number]
        held = {**my, **{a: FULL for a in ORDERS[part][:number]}}
        k = 3 + 6 * (number - 1)
        arrived(part, {**held, first: LOW, axis: near(axis, 2)}, k + 4)
        arrived(part, {**held, first: HIGH, axis: near(axis, 2)}, k + 5)

    everything = (PREFIX, GATE, DOWN, UP)
    for part in everything:
        phase_one(part)

    conv_gain = gains_ref[0:1, :]
    big[0:8, 0:D] = jnp.zeros((8, D), F32)
    big[6:8, 0:D] = edge_ref[...].astype(F32)

    def norm_rows(i, _):
        at = pl.multiple_of(i * 16, 16)
        u = norm(rows_ref[pl.ds(at, 16), :].astype(F32), conv_gain)
        big[pl.ds(pl.multiple_of(at + 8, 8), 16), 0:D] = u.astype(BF).astype(F32)
        return 0

    lax.fori_loop(0, T // 16, norm_rows, 0)
    for part in everything:
        phase_one_on(part)

    def gated(rows, u, one, two):
        convolved = taps_ref[0:1, :] * u + taps_ref[1:2, :] * one + taps_ref[2:3, :] * two
        mixed = (rows.astype(F32) + convolved * jax.nn.sigmoid(u)).astype(BF)
        return mixed, norm(mixed.astype(F32), gains_ref[1:2, :]).astype(BF)

    def conv_rows(i, _):
        at = pl.multiple_of(i * 16, 16)
        window = big[pl.ds(at, 24), 0:D]
        mixed, normed = gated(
            rows_ref[pl.ds(at, 16), :], window[8:], pltpu.roll(window, 1, 0)[8:], pltpu.roll(window, 2, 0)[8:])
        conv[pl.ds(at, 16), :] = mixed
        ain[pl.ds(at, 16), :] = normed
        return 0

    lax.fori_loop(0, T // 16, conv_rows, 0)
    slot_rows[...] = jnp.zeros_like(slot_rows)
    slot_rows[0, 0:4, :] = slots_ref[...].astype(F32)
    for n in range(4):
        before = slot_edge_ref[n].astype(F32)
        slot_rows[2, n:n + 1, :] = before[0:1]
        slot_rows[1, n:n + 1, :] = before[1:2]
    slot_u = norm(slot_rows[0], conv_gain).astype(BF).astype(F32)
    mixed, normed = gated(slot_rows[0], slot_u, slot_rows[1], slot_rows[2])
    conv[T:R, :] = mixed
    ain[T:R, :] = normed

    for part in everything:
        phase_one_end(part)
        phase(part, 1)

    local[0].wait()
    qk[...] = dot(ain[...], wf[...]).astype(BF)
    local[1].wait()

    def value_columns(j, _):
        at = pl.multiple_of(j * 256, 256)
        big[0:R, pl.ds(at, 256)] = dot(ain[...], wv[:, pl.ds(at, 256)]).astype(BF).astype(F32)
        return 0

    lax.fori_loop(0, 3, value_columns, 0)
    for part in everything:
        phase_on(part, 1)
    lax.fori_loop(3, 7, value_columns, 0)

    lane = iota((256, 256), 1)
    feature = iota((256, 256), 0) & 15
    rep[:, 0:256] = (feature == lane >> 4).astype(F32).astype(BF)
    rep[:, 256:512] = (feature == (lane & 15)).astype(F32).astype(BF)

    wide = iota((256, 384), 1)
    deep = iota((256, 384), 0) & 15
    first_sel = jnp.where(wide < 17, wide - 1, (wide - 17) >> 4)
    first_sel = ((deep == first_sel) & (wide < NF)).astype(F32).astype(BF)
    second_sel = ((deep == ((wide - 17) & 15)) & (wide >= 17) & (wide < NF)).astype(F32).astype(BF)
    column = iota((16, 384), 1)
    first_add = (column == 0).astype(F32)
    second_add = jnp.where(column == 0, 1.0, jnp.where(column < 17, FD ** (-0.25), 0.0))
    head_of = (iota((16, 256), 1) >> 4) == iota((16, 256), 0)
    head_start = iota((16, D), 0) * DV
    value_col = iota((16, D), 1)
    head_cols = (value_col >= head_start) & (value_col < head_start + DV)
    slot_qk = qk[T:R, :].astype(F32)
    slot_v = big[T:R, 0:D]
    slot_att[...] = jnp.zeros_like(slot_att)
    sums_row[...] = jnp.zeros_like(sums_row)
    for n in range(4):
        cache_copies[n].wait()
        q = jnp.where(head_of, slot_qk[n:n + 1, 0:256], 0.0)
        s = jnp.sum(q * slot_qk[n:n + 1, 256:512], axis=-1, keepdims=True) * FD ** (-0.5)
        weight = 1.0 + s + 0.5 * s * s
        qb = q.astype(BF)
        phi = (dot(qb, first_sel) + first_add) * (dot(qb, second_sel) * (2.0 * FD) ** (-0.5) + second_add)
        rest = jnp.where(column == 0, 0.0, phi)[:, 0:NF]
        sums_row[:, 0:NF - 1] = keysum_ref[n]
        sums = pltpu.roll(sums_row[...], 1, 1)[:, 0:NF]
        den = jnp.sum(rest * sums, axis=-1, keepdims=True) + length_ref[n].astype(F32) + weight
        phi_high = phi.astype(BF)
        num = dot(phi_high[:, 0:NF], cache[n % 2].astype(BF))
        if n + 2 < 4:
            cache_copies[n + 2].start()
        heads = (num + weight * slot_v[n:n + 1, :]) / den
        slot_att[n:n + 1, 0:D] = jnp.sum(jnp.where(head_cols, heads, 0.0), axis=0, keepdims=True)

    for part in everything:
        phase_near(part, 1)
        phase_far(part, 1)
        if part != PREFIX:
            phase(part, 2)

    for z in range(4):
        for y in range(4):
            h = z * 4 + y
            rep[h * 16:h * 16 + 16, 512:640] = prefix[z, y, 256:272, :]
    big[R:2 * R, 0:D] = jnp.zeros((R, D), F32)
    local[2].wait()
    wo[D:D + 32, :] = jnp.zeros((32, D), BF)
    causal = iota((T, T), 1) <= iota((T, T), 0)
    lane_head = iota((T, 256), 1) >> 4
    lane128 = iota((T, 128), 1)

    def one_head(h):
        qm = jnp.where(lane_head == h, qk[0:T, 0:256].astype(F32), 0.0).astype(BF)
        s = dot_t(qm, qk[0:T, 256:512]) * FD ** (-0.5)
        w = jnp.where(causal, 1.0 + s + 0.5 * s * s, 0.0).astype(BF)
        start = (h * DV // 128) * 128
        window = big[0:T, pl.ds(pl.multiple_of(start, 128), 256)]
        v = pltpu.roll(window, lax.rem(256 + start - h * DV, 256), 1)[:, 0:128]
        v = jnp.where(lane128 < DV, v, jnp.where(lane128 == DV, 1.0, 0.0)).astype(BF)
        phi = (dot(qm, rep[:, 0:256]) * dot(qm, rep[:, 256:512])).astype(BF)
        state = prefix[h // 4, lax.rem(h, 4)]
        num = dot(w, v) + dot(phi, state[0:256]) + dot(qm, rep[:, 512:640]) + state[272:273].astype(F32)
        return jnp.where(lane128 < DV, num / num[:, DV:DV + 1], 0.0)

    lane256 = iota((T, 256), 1)

    def head_pair(p, _):
        left = one_head(2 * p)
        right = one_head(2 * p + 1)
        both = jnp.concatenate([left, jnp.zeros_like(left)], axis=1)
        both = both + pltpu.roll(jnp.concatenate([right, jnp.zeros_like(right)], axis=1), DV, 1)
        pair[0:T, :] = both.astype(BF)
        start = (p * 224 // 128) * 128
        slots = pltpu.roll(slot_att[:, pl.ds(pl.multiple_of(start, 128), 384)], lax.rem(384 + start - p * 224, 384), 1)
        pair[T:R, :] = jnp.where(lane256[0:16] < 224, slots[:, 0:256], 0.0).astype(BF)
        at = pl.multiple_of(p * 224, 32)
        big[R:2 * R, 0:D] += dot(pair[...], wo[pl.ds(at, 256), :])
        return 0

    lax.fori_loop(0, 4, head_pair, 0)
    lax.fori_loop(4, 8, head_pair, 0)

    def hidden_rows(i, _):
        at = pl.multiple_of(i * 16, 16)
        mixed = (conv[pl.ds(at, 16), :].astype(F32) + big[pl.ds(pl.multiple_of(R + at, 16), 16), 0:D]).astype(BF)
        attended[pl.ds(at, 16), :] = mixed
        tok[core, pl.ds(at, 16), :] = norm(mixed.astype(F32), gains_ref[2:3, :]).astype(BF)
        return 0

    lax.fori_loop(0, R // 16, hidden_rows, 0)
    swap = pltpu.make_async_remote_copy(
        tok.at[core], tok.at[core], swap_send.at[0], swap_recv.at[0], device_id={"c": other}, device_id_type=MESH)
    swap.start()
    for part in (GATE, DOWN, UP):
        phase_on(part, 2)
    swap.wait_send()
    pltpu.make_async_remote_copy(
        tok.at[other], tok.at[other], swap_send.at[0], swap_recv.at[0],
        device_id={"c": other}, device_id_type=MESH).wait_recv()
    for part in (GATE, DOWN, UP):
        phase_near(part, 2)
        phase_far(part, 2)

    lane_half = iota((2 * R, 128), 1)

    def feed(x, _):
        tokens = tok[...].reshape(2 * R, D)
        first = dot(tokens, gate[x].reshape(D, 512))
        second = dot(tokens, up[x].reshape(D, 384))
        hid[x, :, 0:384] = (jax.nn.silu(first[:, 0:384]) * second).astype(BF)
        last = first[:, 384:512]
        last = jax.nn.silu(last) * pltpu.roll(last, 64, 1)
        hid[x, :, 384:512] = jnp.where(lane_half < 64, last, 0.0).astype(BF)
        return 0

    lax.fori_loop(0, 4, feed, 0)

    def contract(j, _):
        lanes = pl.ds(pl.multiple_of(j * 256, 256), 256)
        total = dot(hid[0, :, 0:448], down[0, :, lanes])
        for x in range(1, 4):
            total += dot(hid[x, :, 0:448], down[x, :, lanes])
        big[:, lanes] = total
        return 0

    lax.fori_loop(0, 8, contract, 0)

    give[...] = big[pl.ds(pl.multiple_of(other * R, 16), R), :].astype(BF)
    swap = pltpu.make_async_remote_copy(
        give, take, swap_send.at[1], swap_recv.at[1], device_id={"c": other}, device_id_type=MESH)
    swap.start()
    fin[:, 0:D] = attended[...].astype(F32)
    fin[:, D:D + 128] = jnp.zeros((R, 128), F32)
    swap.wait()
    mine = pl.multiple_of(core * R, 16)
    for r in range(H):
        lanes = ((r % 4) * 4 + r // 4) * 128
        piece = big[pl.ds(mine, R), lanes:lanes + 128] + take[:, lanes:lanes + 128].astype(F32)
        start = r * DV // 128 * 128
        piece = pltpu.roll(jnp.concatenate([piece, jnp.zeros_like(piece)], axis=1), r * DV - start, 1)
        fin[:, start:start + 256] += piece
    out_ref[...] = fin[0:T, 0:D].astype(BF)
    live = iota((4, D), 0)
    for n in range(4):
        live = jnp.where(iota((4, D), 0) == n, live_ref[n], live)
    slot_out_ref[...] = jnp.where(live == 1, fin[T:T + 4, 0:D], 0.0).astype(BF)
    for copy in started:
        copy.wait_send()


def on_device(
    prompt_rows, prompt_edge, decode_rows, decode_edge, decode_live, cache_length, cache_state,
    cache_keysum, prefix_length, prefix_state, prefix_keysum, conv_gain, conv_taps, attend_gain,
    feature_weight, value_weight, output_weight, hidden_gain, gate_up, down_weight,
):
    state_in = jnp.pad(prefix_state[0], ((0, 15), (0, 16)))
    keysum = jnp.transpose(cache_keysum, (0, 2, 1))
    gains = jnp.stack([conv_gain, attend_gain, hidden_gain])
    vmem = pl.BlockSpec(memory_space=pltpu.VMEM)
    smem = pl.BlockSpec(memory_space=pltpu.SMEM)
    hbm = pl.BlockSpec(memory_space=pl.ANY)
    return pl.pallas_call(
        layer_kernel,
        out_shape=(jax.ShapeDtypeStruct((T, D), BF), jax.ShapeDtypeStruct((4, D), BF)),
        in_specs=[vmem] * 9 + [smem] * 3 + [vmem] * 2 + [hbm] * 4,
        out_specs=(vmem, vmem),
        scratch_shapes=[
            pltpu.VMEM((4, 4, 4, 112, 512), BF),
            pltpu.VMEM((4, 448, 2048), BF),
            pltpu.VMEM((4, 4, 4, 112, 384), BF),
            pltpu.VMEM((4, 4, 288, 128), BF),
            pltpu.VMEM((D, 512), BF),
            pltpu.VMEM((D, D), BF),
            pltpu.VMEM((D + 32, D), BF),
            pltpu.VMEM((2, NF, D), F32),
            pltpu.VMEM((2 * R, 2048), F32),
            pltpu.VMEM((R, D), BF),
            pltpu.VMEM((R, D), BF),
            pltpu.VMEM((R, 512), BF),
            pltpu.VMEM((256, 640), BF),
            pltpu.VMEM((16, 2048), F32),
            pltpu.VMEM((R, 256), BF),
            pltpu.VMEM((2, R, D), BF),
            pltpu.VMEM((R, D), BF),
            pltpu.VMEM((4, 2 * R, 512), BF),
            pltpu.VMEM((R, 2048), BF),
            pltpu.VMEM((R, 2048), BF),
            pltpu.VMEM((R, D + 128), F32),
            pltpu.VMEM((3, 16, D), F32),
            pltpu.VMEM((448, 128), F32),
            pltpu.VMEM((16, 384), F32),
            pltpu.SemaphoreType.DMA((3,)),
            pltpu.SemaphoreType.DMA((4,)),
            pltpu.SemaphoreType.DMA((4, 15)),
            pltpu.SemaphoreType.DMA((4, 15)),
            pltpu.SemaphoreType.DMA((2,)),
            pltpu.SemaphoreType.DMA((2,)),
        ],
        compiler_params=pltpu.CompilerParams(
            collective_id=0, has_side_effects=True, vmem_limit_bytes=67043328),
    )(
        prompt_rows, prompt_edge[0], decode_rows, decode_edge, keysum, gains, conv_taps,
        state_in, jnp.transpose(prefix_keysum[0]), prefix_length, cache_length, decode_live,
        gate_up, down_weight, jnp.transpose(cache_state, (1, 0, 2)), feature_weight, value_weight,
        output_weight,
    )


def solution(mesh):
    torus = Mesh(mesh.devices.reshape(4, 4, 4, 2), ("z", "y", "x", "c"))
    rows, req, mlp = ("z", "y", "x", "c"), ("z", "y"), ("x", "c")
    return jax.shard_map(
        on_device,
        mesh=torus,
        in_specs=(
            P(rows, None), P(rows, None, None), P(rows, None), P(rows, None, None), P(rows), P(rows),
            P(rows, None, None), P(rows, None, None), P(mlp), P(mlp, None, req), P(mlp, None, req),
            P(), P(), P(), P(), P(), P(), P(), P(None, req, mlp), P(mlp, req),
        ),
        out_specs=(P(rows, None), P(rows, None)),
        check_vma=False,
    )
```
